128 devices in a mesh: img: 16 (over x_lo, z, core), tea: 8 (over y, x_hi).
Axes of the slice: x: 4 (x_hi: 2, x_lo: 2; x = x_hi * 2 + x_lo), y: 4, z: 4, core: 2. Of those that a mesh axis runs over, the one named last changes fastest.
Arguments:
- student: bfloat16 [16384, 1280], P(('img', 'tea')), may hold values from -6 to 6
- w_in: bfloat16 [8, 1280, 1280], P('tea'), may hold values from -0.15625 to 0.15625
- w_out: bfloat16 [8, 1280, 1280], P('tea'), may hold values from -0.15625 to 0.15625
- target: bfloat16 [8, 16384, 1280], P('tea', 'img'), may hold values from -6 to 6
Outputs:
- grad_student: bfloat16 [16384, 1280], P(('img', 'tea'))
- grad_in: bfloat16 [8, 1280, 1280], P('tea')
- grad_out: bfloat16 [8, 1280, 1280], P('tea')
The draws below stay inside these ranges and needn't reach their ends.
All inputs are finite; a program needn't handle non-finite values.
Results may differ from the reference program's by a relative error of at most 0.015.
Values may be sent and summed in bfloat16 or wider, within the bound.
No kernel may reach another device: no remote copies, remote signals or barrier semaphores. Data moves between devices by JAX's collectives and lax.ppermute only.
A program may use at most 128 MiB of HBM per device.

```python
import jax
import jax.numpy as jnp
from jax import lax

D = 1280
H = 1280
TOKENS = 16384
TEACHERS = 8


def level_of(key, shape, pieces, least, top_value):
    level = 1.0
    for dim, shards_of in pieces:
        draws = jax.random.uniform(jax.random.fold_in(jax.random.fold_in(key, 6), dim), (shards_of,), jnp.float32, least / len(pieces), top_value / len(pieces))
        level = level * jnp.repeat(jnp.exp(draws), shape[dim] // shards_of).reshape((-1,) + (1,) * (len(shape) - 1 - dim))
    return level


def scatter_about(stream_key, dims, spread, limit, pieces=(), dtype=jnp.bfloat16):
    drawn = spread * jax.random.normal(stream_key, dims, jnp.float32)
    if pieces:
        drawn = drawn * level_of(stream_key, dims, pieces, -0.22, 0.18)
    return jnp.clip(drawn, -limit, limit).astype(dtype)


def setup_inputs(seed: int = 0) -> dict:
    keys = jax.random.split(jax.random.key(seed), 5)
    student = scatter_about(keys[0], (TOKENS, D), 1.0, 6.0, ((0, 128),))
    w_in = scatter_about(keys[1], (TEACHERS, D, H), D ** -0.5, 0.15625, ((0, 8),))
    w_out = scatter_about(keys[2], (TEACHERS, H, H), H ** -0.5, 0.15625, ((0, 8),))
    target = scatter_about(keys[3], (TEACHERS, TOKENS, H), 1.0, 6.0, ((0, 8), (1, 16)))
    return {"student": student, "w_in": w_in, "w_out": w_out, "target": target}


def gelu_parts(pre):
    cdf = 0.5 * (1.0 + lax.erf(pre * 0.7071067811865476))
    pdf = jnp.exp(-0.5 * pre * pre) * 0.3989422804014327
    return (pre * cdf, cdf + pre * pdf)

def reference(student, w_in, w_out, target):
    scale = 1.0 / jnp.sqrt(jnp.float32(TOKENS))

    def teacher(carry, items):
        first, second, goal = items
        pre = jnp.dot(student, first, preferred_element_type=jnp.float32)
        value, slope_factor = gelu_parts(pre)
        hidden = value.astype(jnp.bfloat16)
        pred = jnp.dot(hidden, second, preferred_element_type=jnp.float32)
        err = (pred - goal.astype(jnp.float32)).astype(jnp.bfloat16)
        back = jnp.dot(err, second.T, preferred_element_type=jnp.float32)
        slope = (back * slope_factor).astype(jnp.bfloat16)
        carry = carry + jnp.dot(slope, first.T, preferred_element_type=jnp.float32)
        grad_first = (jnp.dot(student.T, slope, preferred_element_type=jnp.float32) * scale).astype(jnp.bfloat16)
        grad_second = (jnp.dot(hidden.T, err, preferred_element_type=jnp.float32) * scale).astype(jnp.bfloat16)
        return (carry, (grad_first, grad_second))
    start = jnp.zeros((TOKENS, D), jnp.float32)
    total, grads = lax.scan(teacher, start, (w_in, w_out, target))
    grad_student = (total / TEACHERS).astype(jnp.bfloat16)
    return (grad_student, grads[0], grads[1])
```

```python
import jax
import jax.numpy as jnp
from jax import lax
from jax.sharding import PartitionSpec as P


F32 = jnp.float32
BF16 = jnp.bfloat16
AXES = ("img", "tea")


def place(x, y, z, c):
    return (((x % 2) * 4 + z) * 2 + c) * 8 + y * 2 + x // 2


def pairs(move):
    return [
        (place(x, y, z, c), place(*move(x, y, z, c)))
        for x in range(4)
        for y in range(4)
        for z in range(4)
        for c in range(2)
    ]


def near(v, c):
    return v ^ 1 if c == 0 else 3 - v


def far(v, c):
    return 3 - v if c == 0 else v ^ 1


Y1 = pairs(lambda x, y, z, c: (x, near(y, c), z, c))
Y2 = pairs(lambda x, y, z, c: (x, far(y, c), z, c))
Z1 = pairs(lambda x, y, z, c: (x, y, near(z, c), c))
Z2 = pairs(lambda x, y, z, c: (x, y, far(z, c), c))
XT = pairs(lambda x, y, z, c: ((x + 2) % 4, y, z, c))
XI = pairs(lambda x, y, z, c: (x ^ 1, y, z, c))
CORE = pairs(lambda x, y, z, c: (x, y, z, 1 - c))


def move(a, where):
    return lax.ppermute(a, AXES, where)


def gelu_parts(pre):
    cdf = 0.5 * (1.0 + lax.erf(pre * 0.7071067811865476))
    pdf = jnp.exp(-0.5 * pre * pre) * 0.3989422804014327
    return (pre * cdf, cdf + pre * pdf)


def dot(a, b, da, db):
    return lax.dot_general(a, b, (((da,), (db,)), ((), ())), preferred_element_type=F32)


def part(a, k):
    n = a.shape[0] // 2
    return lax.dynamic_slice_in_dim(a, k * n, n, 0)


def swap_sum(total, bit, where):
    got = move(part(total, 1 - bit).astype(BF16), where)
    return part(total, bit) + got.astype(F32)


def swap_join(mine, bit, where):
    got = move(mine, where)
    n = mine.shape[0]
    return lax.dynamic_slice_in_dim(jnp.concatenate([got, mine, got], 0), (1 - bit) * n, 2 * n, 0)


def summed_over_images(lhs, rhs, scale, c, bits):
    width = lhs.shape[1] // 2
    half = lambda k: dot(lax.dynamic_slice_in_dim(lhs, k * width, width, 1), rhs, 0, 0)
    got = move(half(1 - c).astype(BF16), CORE)
    total = half(c) + got.astype(F32)
    stages = list(zip(bits, (Z1, Z2, XI)))
    for bit, where in stages:
        total = swap_sum(total, bit, where)
    mine = (total * scale).astype(BF16)
    for bit, where in reversed(stages):
        mine = swap_join(mine, bit, where)
    return swap_join(mine, c, CORE)


def shards(student, w_in, w_out, target):
    img, tea = lax.axis_index("img"), lax.axis_index("tea")
    c, z, xl = img % 2, (img // 2) % 4, img // 8
    y, xh = tea // 2, tea % 2
    rows = student.shape[0]
    first, second = w_in[0], w_out[0]

    ox = move(student, XT)
    f, n = move(student, Y2), move(student, Y1)
    a = move(f, Y1)
    fx, nx = move(ox, Y2), move(ox, Y1)
    ax = move(a, XT)
    whole = jnp.concatenate([student, ox, f, fx, n, nx, a, ax], 0)
    yn = jnp.where(c == 0, y ^ 1, 3 - y)
    yf = jnp.where(c == 0, 3 - y, y ^ 1)
    ya = (y + 2) % 4
    goal = jnp.concatenate(
        [
            lax.dynamic_slice_in_dim(target[0], (v * 2 + h) * rows, rows, 0)
            for v in (y, yf, yn, ya)
            for h in (xh, 1 - xh)
        ],
        0,
    )

    pre = dot(whole, first, 1, 0)
    value, slope_factor = gelu_parts(pre)
    hidden = value.astype(BF16)
    pred = dot(hidden, second, 1, 0)
    err = (pred - goal.astype(F32)).astype(BF16)
    scale = 1.0 / jnp.sqrt(F32(whole.shape[0] * lax.axis_size("img")))
    gray = (z ^ (z // 2)) % 2
    bits = (jnp.where(c == 0, gray, z // 2), jnp.where(c == 0, z // 2, z % 2), xl)
    grad_out = summed_over_images(hidden, err, scale, c, bits)
    back = dot(err, second, 1, 1)
    slope = (back * slope_factor).astype(BF16)
    grad_in = summed_over_images(whole, slope, scale, c, bits)

    half = whole.shape[0] // 2
    got = move(dot(slope[half:], first, 1, 1).astype(BF16), Y1)
    total = dot(slope[:half], first, 1, 1) + got.astype(F32)
    for where in (Y2, XT):
        half = half // 2
        total = total[:half] + move(total[half:].astype(BF16), where).astype(F32)
    grad_student = (total / lax.axis_size("tea")).astype(BF16)
    return (grad_student, grad_in[None], grad_out[None])


def solution(mesh):
    return jax.shard_map(
        shards,
        mesh=mesh,
        in_specs=(
            P(("img", "tea"), None),
            P("tea", None, None),
            P("tea", None, None),
            P("tea", "img", None),
        ),
        out_specs=(P(("img", "tea"), None), P("tea", None, None), P("tea", None, None)),
        check_vma=False,
    )
```

```python
import functools

import jax
import jax.numpy as jnp
import numpy as np
from jax import lax
from jax.experimental import pallas as pl
from jax.experimental.pallas import tpu as pltpu
from jax.sharding import PartitionSpec as P


F32 = jnp.float32
BF16 = jnp.bfloat16
AXES = ("img", "tea")
MIB = 1 << 20


def place(x, y, z, c):
    return (((x % 2) * 4 + z) * 2 + c) * 8 + y * 2 + x // 2


SPOTS = [(x, y, z, c) for x in range(4) for y in range(4) for z in range(4) for c in range(2)]


def pairs(move):
    return [(place(*s), place(*move(*s))) for s in SPOTS]


def near(v, c):
    return v ^ 1 if c == 0 else 3 - v


def far(v, c):
    return 3 - v if c == 0 else v ^ 1


Y1 = pairs(lambda x, y, z, c: (x, near(y, c), z, c))
Y2 = pairs(lambda x, y, z, c: (x, far(y, c), z, c))
Z1 = pairs(lambda x, y, z, c: (x, y, near(z, c), c))
Z2 = pairs(lambda x, y, z, c: (x, y, far(z, c), c))
XT = pairs(lambda x, y, z, c: ((x + 2) % 4, y, z, c))
XI = pairs(lambda x, y, z, c: (x ^ 1, y, z, c))
CORE = pairs(lambda x, y, z, c: (x, y, z, 1 - c))


def bits_of(x, z, c):
    first = ((z ^ (z >> 1)) & 1, z >> 1)[c]
    second = (z >> 1, z & 1)[c]
    return first, second, x % 2


TABLE = np.zeros((128, 20), np.int32)
for x, y, z, c in SPOTS:
    h = x // 2
    own, ox = y * 2 + h, y * 2 + 1 - h
    f, n, a = far(y, c), near(y, c), y ^ 2
    b1, b2, b3 = bits_of(x, z, c)
    o1 = bits_of(x, z, 1 - c)[0]
    TABLE[place(x, y, z, c)] = [
        own, ox, f * 2 + h, n * 2 + h, f * 2 + 1 - h, n * 2 + 1 - h, a * 2 + h, a * 2 + 1 - h,
        c, b1, b2, b3,
        b2 * 2 + b3, b2 * 2 + 1 - b3, (1 - b2) * 2 + b3, (1 - b2) * 2 + 1 - b3,
        c * 2 + b1, c * 2 + 1 - b1, (1 - c) * 2 + o1, (1 - c) * 2 + 1 - o1,
    ]


def move(a, where):
    return lax.ppermute(a, AXES, where)


def gelu_parts(pre):
    cdf = 0.5 * (1.0 + lax.erf(pre * 0.7071067811865476))
    pdf = jnp.exp(-0.5 * pre * pre) * 0.3989422804014327
    return (pre * cdf, cdf + pre * pdf)


def dot(a, b, da, db):
    return lax.dot_general(a, b, (((da,), (db,)), ((), ())), preferred_element_type=F32)


def heads_kernel(tab, p0, p1, p2, p3, t0, t1, t2, t3, w1, w2, rows, hid, err, slope):
    pieces, goals = (p0, p1, p2, p3), (t0, t1, t2, t3)
    n = p0.shape[0]
    for k in (0, 2):
        at = pl.ds(k * n, 2 * n)
        x = jnp.concatenate([pieces[k][...], pieces[k + 1][...]], 0)
        goal = jnp.concatenate([goals[k][0], goals[k + 1][0]], 0)
        rows[at, :] = x
        value, factor = gelu_parts(dot(x, w1[...], 1, 0))
        hidden = value.astype(BF16)
        hid[at, :] = hidden
        e = (dot(hidden, w2[...], 1, 0) - goal.astype(F32)).astype(BF16)
        err[at, :] = e
        slope[at, :] = (dot(e, w2[...], 1, 1) * factor).astype(BF16)


def heads(tab, k, pieces, target, w1, w2):
    n, d = pieces[0].shape
    m = 4 * n
    whole = lambda s: pl.BlockSpec(s, lambda g, tab: (0,) * len(s))
    goal = lambda j: pl.BlockSpec((1, n, d), lambda g, tab: (0, tab[k + j], 0))
    out = jax.ShapeDtypeStruct((m, d), BF16)
    return pl.pallas_call(
        heads_kernel,
        grid_spec=pltpu.PrefetchScalarGridSpec(
            num_scalar_prefetch=1,
            grid=(1,),
            in_specs=[whole((n, d))] * 4 + [goal(j) for j in range(4)] + [whole(w1.shape), whole(w2.shape)],
            out_specs=[whole((m, d))] * 4,
        ),
        out_shape=[out] * 4,
        compiler_params=pltpu.CompilerParams(vmem_limit_bytes=40 * MIB),
        cost_estimate=pl.CostEstimate(flops=6 * m * d * d, bytes_accessed=14 * MIB, transcendentals=2 * m * d),
        name="heads",
    )(tab, *pieces, target, target, target, target, w1, w2)


def join_kernel(at, tab, *refs):
    *parts, out = refs
    n = parts[0].shape[0]
    for k, ref in enumerate(parts):
        out[pl.ds(pl.multiple_of(tab[at + k] * n, 16), n), :] = ref[...]


def join(tab, at, parts):
    n, d = parts[0].shape
    k = len(parts)
    return pl.pallas_call(
        functools.partial(join_kernel, at),
        grid_spec=pltpu.PrefetchScalarGridSpec(
            num_scalar_prefetch=1,
            grid=(1,),
            in_specs=[pl.BlockSpec((n, d), lambda g, tab: (0, 0))] * k,
            out_specs=pl.BlockSpec((k * n, d), lambda g, tab: (0, 0)),
        ),
        out_shape=jax.ShapeDtypeStruct((k * n, d), BF16),
        compiler_params=pltpu.CompilerParams(vmem_limit_bytes=16 * MIB),
        cost_estimate=pl.CostEstimate(flops=0, bytes_accessed=4 * k * n * d, transcendentals=0),
        name="join",
    )(tab, *parts)


def part(a, k):
    n = a.shape[0] // 2
    return lax.dynamic_slice_in_dim(a, k * n, n, 0)


def swap_sum(total, bit, where):
    got = move(part(total, 1 - bit).astype(BF16), where)
    return part(total, bit) + got.astype(F32)


def summed_over_images(lhs, rhs, scale, tab):
    width = lhs[0].shape[1] // 2
    cut = lambda a, k: lax.dynamic_slice_in_dim(a, k * width, width, 1)
    half = lambda k: sum(dot(cut(a, k), b, 0, 0) for a, b in zip(lhs, rhs))
    c = tab[8]
    got = move(half(1 - c).astype(BF16), CORE)
    total = half(c) + got.astype(F32)
    for k, where in enumerate((Z1, Z2, XI)):
        total = swap_sum(total, tab[9 + k], where)
    mine = (total * scale).astype(BF16)
    x, z = move(mine, XI), move(mine, Z2)
    block = join(tab, 12, [mine, x, z, move(x, Z2)])
    other = move(block, Z1)
    return join(tab, 16, [block, other, move(block, CORE), move(other, CORE)])


def shards(student, w_in, w_out, target):
    tab = lax.dynamic_index_in_dim(
        jnp.asarray(TABLE), lax.axis_index("img") * 8 + lax.axis_index("tea"), 0, keepdims=False
    )
    first, second = w_in[0], w_out[0]

    f, n = move(student, Y2), move(student, Y1)
    ox = move(student, XT)
    a = move(f, Y1)
    fx, nx = move(ox, Y2), move(ox, Y1)
    ax = move(a, XT)
    runs = [
        heads(tab, 0, (student, ox, f, n), target, first, second),
        heads(tab, 4, (fx, nx, a, ax), target, first, second),
    ]
    rows, hidden, err, slope = zip(*runs)
    scale = 1.0 / jnp.sqrt(F32(8 * student.shape[0] * lax.axis_size("img")))
    grad_out = summed_over_images(hidden, err, scale, tab)
    grad_in = summed_over_images(rows, slope, scale, tab)

    m = student.shape[0]
    lower, upper = slope
    away = jnp.concatenate([lower[3 * m :], upper[m:]], 0)
    kept = jnp.concatenate([lower[: 3 * m], upper[:m]], 0)
    got = move(dot(away, first, 1, 1).astype(BF16), Y1)
    total = dot(kept, first, 1, 1) + got.astype(F32)
    half = 4 * m
    for where in (Y2, XT):
        half = half // 2
        total = total[:half] + move(total[half:].astype(BF16), where).astype(F32)
    grad_student = (total / lax.axis_size("tea")).astype(BF16)
    return (grad_student, grad_in[None], grad_out[None])


def solution(mesh):
    return jax.shard_map(
        shards,
        mesh=mesh,
        in_specs=(
            P(("img", "tea"), None),
            P("tea", None, None),
            P("tea", None, None),
            P("tea", "img", None),
        ),
        out_specs=(P(("img", "tea"), None), P("tea", None, None), P("tea", None, None)),
        check_vma=False,
    )
```
